32 devices in a mesh: tm: 4 (over y, core), space: 8 (over z, x).
Axes of the slice: x: 2, y: 2, z: 4, core: 2. Of those that a mesh axis runs over, the one named last changes fastest.
Arguments:
- latent: bfloat16 [32, 32, 64, 256], P('tm', 'space'), may hold values from -6 to 6
- spatial_weight: bfloat16 [3, 3, 256, 256], replicated, may hold values from -0.125 to 0.125
- spatial_bias: float32 [256], replicated, may hold values from -3 to 3
- temporal_weight: bfloat16 [3, 256, 256], replicated, may hold values from -0.21875 to 0.21875
- temporal_bias: float32 [256], replicated, may hold values from -3 to 3
Outputs:
- upsampled: bfloat16 [32, 64, 128, 256], P(('tm', 'space'))
The draws below stay inside these ranges and needn't reach their ends.
All inputs are finite; a program needn't handle non-finite values.
Results may differ from the reference program's by a relative error of at most 0.0032.
Values may be sent and summed in bfloat16 or wider, within the bound.
No kernel may reach another device: no remote copies, remote signals or barrier semaphores. Data moves between devices by JAX's collectives and lax.ppermute only.
A program may use at most 128 MiB of HBM per device.

```python
import jax
import jax.numpy as jnp
from jax import lax

C = 256
W = 64
FRAMES = 32
H = 32


def shard_levels(stream_key, dims, split, least, high):
    def one(dim, blocks):
        steps = jax.random.uniform(jax.random.fold_in(jax.random.fold_in(stream_key, 6), dim), (blocks,), jnp.float32, least / len(split), high / len(split))
        return jnp.repeat(jnp.exp(steps), dims[dim] // blocks).reshape((-1,) + (1,) * (len(dims) - dim - 1))

    gain = one(*split[0])
    for cut in split[1:]:
        gain = gain * one(*cut)
    return gain


def normal_values(rng, extent, scale, most, pieces=(), kind=jnp.bfloat16):
    values = jax.random.normal(rng, extent, jnp.float32) * scale
    if len(pieces) > 0:
        values = shard_levels(rng, extent, pieces, -0.22, 0.18) * values
    return jnp.clip(values, min=-most, max=most).astype(kind)


def setup_inputs(seed: int = 0) -> dict:
    key_of = jax.random.split(jax.random.key(seed), 6)
    return {
        "latent": normal_values(key_of[0], (FRAMES, H, W, C), 1.0, 6.0, ((0, 4), (1, 8))),
        "spatial_weight": normal_values(key_of[1], (3, 3, C, C), (9 * C) ** -0.5, 0.125),
        "spatial_bias": normal_values(key_of[2], (C,), 0.5, 3.0, (), jnp.float32),
        "temporal_weight": normal_values(key_of[3], (3, C, C), (3 * C) ** -0.5, 0.21875),
        "temporal_bias": normal_values(key_of[4], (C,), 0.5, 3.0, (), jnp.float32),
    }


def spatial_frame(frame, spatial_weight, spatial_bias):
    rows = frame.shape[0]
    cols = frame.shape[1]
    chans = frame.shape[2]
    padded = jnp.pad(frame, ((1, 1), (1, 1), (0, 0)))
    total = jnp.zeros((rows * cols, chans), jnp.float32)
    for a in range(3):
        for b in range(3):
            tile = padded[a:a + rows, b:b + cols, :].reshape(rows * cols, chans)
            total = total + jnp.dot(tile, spatial_weight[a, b], preferred_element_type=jnp.float32)
    total = total + spatial_bias
    return jax.nn.silu(total).astype(jnp.bfloat16).reshape(rows, cols, chans)


def reference(latent, spatial_weight, spatial_bias, temporal_weight, temporal_bias):
    frames, rows, cols, chans = latent.shape
    hidden = lax.map(lambda frame: spatial_frame(frame, spatial_weight, spatial_bias), latent)
    padded = jnp.concatenate([jnp.zeros((2, rows, cols, chans), jnp.bfloat16), hidden], axis=0)

    def temporal_frame(index):
        total = jnp.zeros((rows * cols, chans), jnp.float32)
        for k in range(3):
            piece = lax.dynamic_index_in_dim(padded, index + k, 0, keepdims=False).reshape(rows * cols, chans)
            total = total + jnp.dot(piece, temporal_weight[k], preferred_element_type=jnp.float32)
        own = lax.dynamic_index_in_dim(latent, index, 0, keepdims=False).reshape(rows * cols, chans)
        mixed = (own.astype(jnp.float32) + total + temporal_bias).astype(jnp.bfloat16).reshape(rows, cols, chans)
        grown = jnp.broadcast_to(mixed[:, None, :, None, :], (rows, 2, cols, 2, chans))
        return grown.reshape(2 * rows, 2 * cols, chans)

    return lax.map(temporal_frame, jnp.arange(frames, dtype=jnp.int32))
```

```python
import jax
import jax.numpy as jnp
from jax import lax
from jax.experimental import pallas as pl
from jax.experimental.pallas import tpu as pltpu
from jax.sharding import PartitionSpec as P

VMEM = pl.BlockSpec(memory_space=pltpu.VMEM)
ANY = pl.BlockSpec(memory_space=pl.ANY)
MIB = 1 << 20


def activate(taps, weight_ref, bias):
    frames, cols, chans = taps[0].shape
    wide = jnp.concatenate([t.reshape(frames * cols, chans) for t in taps], axis=1)

    def tap(b):
        w = weight_ref[:, b].reshape(3 * chans, chans)
        return jnp.dot(wide, w, preferred_element_type=jnp.float32).reshape(frames, cols, chans)

    col = lax.broadcasted_iota(jnp.int32, (1, cols, chans), 1)
    left = jnp.where(col == 0, 0.0, pltpu.roll(tap(0), 1, axis=1))
    right = jnp.where(col == cols - 1, 0.0, pltpu.roll(tap(2), cols - 1, axis=1))
    v = tap(1) + left + right + bias
    half = 0.5 * v
    return (half + half * jnp.tanh(half)).astype(jnp.bfloat16)


def mix(hidden, own, weight_ref, bias):
    frames, cols, chans = own.shape
    wide = jnp.concatenate([hidden[k : k + frames].reshape(frames * cols, chans) for k in range(3)], axis=1)
    total = jnp.dot(wide, weight_ref[...].reshape(3 * chans, chans), preferred_element_type=jnp.float32)
    return (own.astype(jnp.float32) + total.reshape(frames, cols, chans) + bias).astype(jnp.bfloat16)


def finish(rows, latent_ref, sw_ref, sb_ref, tw_ref, tb_ref, outs, mixed_ref):
    frames = latent_ref.shape[0]
    inside = lax.axis_index("tm") > 0
    me = lax.axis_index("space")
    for i, (r, taps) in enumerate(rows):
        hidden = activate(taps, sw_ref, sb_ref[...])
        first = lax.broadcasted_iota(jnp.int32, hidden.shape, 0) < 2
        hidden = jnp.where(jnp.logical_and(first, jnp.logical_not(inside)), jnp.zeros_like(hidden), hidden)
        mixed_ref[:, i] = mix(hidden, latent_ref[:, r], tw_ref, tb_ref[...])
    for k in range(frames):
        outs[k][...] = mixed_ref[lax.rem(me + k, frames)]


def inner_kernel(latent_ref, prev_ref, sw_ref, sb_ref, tw_ref, tb_ref, *rest):
    outs, mixed_ref = rest[:-1], rest[-1]
    rows = latent_ref.shape[1]

    def row(r):
        return jnp.concatenate([prev_ref[:, r], latent_ref[:, r]], axis=0)

    jobs = [(r, [row(r - 1), row(r), row(r + 1)]) for r in range(1, rows - 1)]
    finish(jobs, latent_ref, sw_ref, sb_ref, tw_ref, tb_ref, outs, mixed_ref)


def edge_kernel(latent_ref, prev_ref, up_ref, down_ref, prev_up_ref, prev_down_ref, sw_ref, sb_ref, tw_ref, tb_ref, *rest):
    outs, mixed_ref = rest[:-1], rest[-1]
    rows = latent_ref.shape[1]

    def row(r):
        if r < 0:
            return jnp.concatenate([prev_up_ref[:, 0], up_ref[:, 0]], axis=0)
        if r == rows:
            return jnp.concatenate([prev_down_ref[:, 0], down_ref[:, 0]], axis=0)
        return jnp.concatenate([prev_ref[:, r], latent_ref[:, r]], axis=0)

    jobs = [(r, [row(r - 1), row(r), row(r + 1)]) for r in (0, rows - 1)]
    finish(jobs, latent_ref, sw_ref, sb_ref, tw_ref, tb_ref, outs, mixed_ref)


def conv_call(kernel, count, frames, cols, chans, args, name):
    shape = (count, cols, chans)
    rows = count * frames * cols
    return pl.pallas_call(
        kernel,
        out_shape=[jax.ShapeDtypeStruct(shape, jnp.bfloat16)] * frames,
        in_specs=[VMEM] * len(args),
        out_specs=[VMEM] * frames,
        scratch_shapes=[pltpu.VMEM((frames,) + shape, jnp.bfloat16)],
        compiler_params=pltpu.CompilerParams(vmem_limit_bytes=32 * MIB),
        cost_estimate=pl.CostEstimate(flops=2 * rows * 12 * chans * chans, transcendentals=rows * chans, bytes_accessed=4 * MIB),
        name=name,
    )(*args)


def grow_kernel(groups, *refs):
    pieces, out_ref, grown_ref, sems = refs[:-4], refs[-3], refs[-2], refs[-1]
    n = len(pieces)
    count, cols, chans = pieces[0].shape
    tile = out_ref.shape[1] // n
    me = lax.axis_index("space")
    at = lax.broadcasted_iota(jnp.int32, (2 * cols, cols), 0)
    of = lax.broadcasted_iota(jnp.int32, (2 * cols, cols), 1)
    twice = jnp.where(at // 2 == of, 1.0, 0.0).astype(jnp.bfloat16)
    copies = []
    for k in range(n):
        src = lax.rem(me + n - k, n)
        for i in range(count):
            wide = jnp.dot(twice, pieces[k][i], preferred_element_type=jnp.float32).astype(jnp.bfloat16)
            grown_ref[k, 2 * i] = wide
            grown_ref[k, 2 * i + 1] = wide
        done = 0
        for g, (first, rows) in enumerate(groups):
            copy = pltpu.make_async_copy(
                grown_ref.at[k, pl.ds(2 * done, 2 * rows)],
                out_ref.at[0, pl.ds(src * tile + 2 * first, 2 * rows)],
                sems.at[k, g],
            )
            copy.start()
            copies.append(copy)
            done += rows
    for copy in copies:
        copy.wait()


def grow_call(groups, pieces, out, height, name):
    n = len(pieces)
    count, cols, chans = pieces[0].shape
    shape = jax.ShapeDtypeStruct((1, 2 * height, 2 * cols, chans), jnp.bfloat16)
    extra = [] if out is None else [out]

    def kernel(*refs):
        grow_kernel(groups, *refs[:n], None, *refs[n + len(extra) :])

    return pl.pallas_call(
        kernel,
        out_shape=shape,
        in_specs=[VMEM] * n + [ANY] * len(extra),
        out_specs=ANY,
        input_output_aliases={n: 0} if extra else {},
        scratch_shapes=[
            pltpu.VMEM((n, 2 * count, 2 * cols, chans), jnp.bfloat16),
            pltpu.SemaphoreType.DMA((n, len(groups))),
        ],
        compiler_params=pltpu.CompilerParams(vmem_limit_bytes=32 * MIB),
        cost_estimate=pl.CostEstimate(flops=0, transcendentals=0, bytes_accessed=2 * n * count * 4 * cols * chans),
        name=name,
    )(*pieces, *extra)


def shifted(block, axis, distance):
    n = lax.axis_size(axis)
    return lax.ppermute(block, axis, [(i, i + distance) for i in range(n) if 0 <= i + distance < n])


def corner(block, distance):
    ts, ss = lax.axis_size("tm"), lax.axis_size("space")
    route = [(t * ss + s, (t + 1) * ss + s + distance) for t in range(ts - 1) for s in range(ss) if 0 <= s + distance < ss]
    return lax.ppermute(block, ("tm", "space"), route)


def exchange(pieces):
    n = len(pieces)
    return [pieces[0]] + [lax.ppermute(pieces[k], "space", [(i, (i + k) % n) for i in range(n)]) for k in range(1, n)]


def body(latent, spatial_weight, spatial_bias, temporal_weight, temporal_bias):
    frames, rows, cols, chans = latent.shape
    n = lax.axis_size("space")
    params = [spatial_weight, spatial_bias.reshape(1, chans), temporal_weight, temporal_bias.reshape(1, chans)]
    head, tail = latent[:, :1], latent[:, rows - 1 :]
    prev = shifted(latent[frames - 2 :], "tm", 1)
    up = shifted(tail, "space", 1)
    down = shifted(head, "space", -1)
    prev_up = corner(tail[frames - 2 :], 1)
    prev_down = corner(head[frames - 2 :], -1)
    inner = conv_call(inner_kernel, rows - 2, frames, cols, chans, [latent, prev] + params, "inner")
    inner = exchange(inner)
    edge = conv_call(edge_kernel, 2, frames, cols, chans, [latent, prev, up, down, prev_up, prev_down] + params, "edge")
    edge = exchange(edge)
    out = grow_call(((1, rows - 2),), inner, None, rows * n, "grow_inner")
    return grow_call(((0, 1), (rows - 1, 1)), edge, out, rows * n, "grow_edge")


def solution(mesh):
    in_specs = (P("tm", "space", None, None), P(), P(), P(), P())
    out_specs = P(("tm", "space"), None, None, None)
    return jax.shard_map(body, mesh=mesh, in_specs=in_specs, out_specs=out_specs, check_vma=False)
```

```python
import jax
import jax.numpy as jnp
from jax import lax
from jax.experimental import pallas as pl
from jax.experimental.pallas import tpu as pltpu
from jax.sharding import PartitionSpec as P

VMEM = pl.BlockSpec(memory_space=pltpu.VMEM)
HBM = pl.BlockSpec(memory_space=pltpu.HBM)
BF16 = jnp.bfloat16
MIB = 1 << 20
PARAMS = pltpu.CompilerParams(vmem_limit_bytes=24 * MIB)


def bf16(*shape):
    return jax.ShapeDtypeStruct(shape, BF16)


def exchanges(n):
    far = sorted(range(n // 2, n), key=lambda k: (k & 1, k))
    cut = 3 * n // 8
    return far[:cut], far[cut:] + sorted(range(1, n // 2), key=lambda k: -k)


def copy_all(pairs, sems):
    copies = [pltpu.make_async_copy(a, b, sems.at[i]) for i, (a, b) in enumerate(pairs)]
    for copy in copies:
        copy.start()
    for copy in copies:
        copy.wait()


def border_kernel(latent, near, far, last, sems):
    frames, rows = latent.shape[:2]
    odd = lax.rem(lax.axis_index("space"), 2)
    near_row, far_row = (rows - 1) * (1 - odd), (rows - 1) * odd
    pairs = [(latent.at[:, near_row], near), (latent.at[:, far_row], far), (latent.at[pl.ds(frames - 2, 2)], last)]
    copy_all(pairs, sems)


def load_kernel(*refs):
    m = len(refs) // 2
    copy_all(list(zip(refs[:m], refs[m : 2 * m])), refs[-1])


def activate(taps, order, weight_ref, bias):
    frames, cols, chans = taps[0].shape
    wide = jnp.concatenate([t.reshape(frames * cols, chans) for t in taps], axis=1)

    def tap(b):
        w = jnp.concatenate([weight_ref[a, b] for a in order], axis=0)
        return jnp.dot(wide, w, preferred_element_type=jnp.float32).reshape(frames, cols, chans)

    col = lax.broadcasted_iota(jnp.int32, (1, cols, chans), 1)
    left = jnp.where(col == 0, 0.0, pltpu.roll(tap(0), 1, axis=1))
    right = jnp.where(col == cols - 1, 0.0, pltpu.roll(tap(2), cols - 1, axis=1))
    half = 0.5 * (tap(1) + left + right + bias)
    return (half + half * jnp.tanh(half)).astype(BF16)


def mix(before, hidden, own, weight_ref, bias):
    frames, cols, chans = own.shape
    before = jnp.where(lax.axis_index("tm") > 0, before, jnp.zeros_like(before))
    joined = jnp.concatenate([before, hidden], axis=0)
    wide = jnp.concatenate([joined[k : k + frames].reshape(frames * cols, chans) for k in range(3)], axis=1)
    total = jnp.dot(wide, weight_ref[...].reshape(3 * chans, chans), preferred_element_type=jnp.float32)
    return (own.astype(jnp.float32) + total.reshape(frames, cols, chans) + bias).astype(BF16)


def inner_kernel(early, latent, prev, sw, sb, tw, tb, mixed, *outs):
    rows = latent.shape[1]
    me = lax.axis_index("space")

    def row(r):
        return jnp.concatenate([prev[:, r], latent[:, r]], axis=0)

    for r in range(1, rows - 1):
        hidden = activate([row(r - 1), row(r), row(r + 1)], (0, 1, 2), sw, sb[...])
        mixed[:, r - 1] = mix(hidden[:2], hidden[2:], latent[:, r], tw, tb[...])
    for k, out in zip(early, outs):
        out[...] = mixed[lax.bitwise_xor(me, k)]


def sides(rows):
    odd = lax.rem(lax.axis_index("space"), 2)
    for top in (odd, 1 - odd):
        yield (rows - 1) * (1 - top), 1 + (rows - 3) * (1 - top), 1 - top, (2 - 2 * top, 1, 2 * top)


def outside(i, halo):
    if i == 0:
        return halo
    me = lax.axis_index("space")
    inside = jnp.logical_and(me > 0, me < lax.axis_size("space") - 1)
    return jnp.where(inside, halo, jnp.zeros_like(halo))


def edge_kernel(latent, near, far, sw, sb, hidden):
    for i, (halo, (r, beyond, _, order)) in enumerate(zip((near, far), sides(latent.shape[1]))):
        hidden[i] = activate([outside(i, halo[...]), latent[:, r], latent[:, beyond]], order, sw, sb[...])


def join_kernel(early, whole, latent, prev, corners, hidden, inner, sw, sb, tw, tb, *rest):
    outs, mixed = rest[:-1], rest[-1]
    rows = latent.shape[1]
    me = lax.axis_index("space")
    for i, (r, beyond, place, order) in enumerate(sides(rows)):
        before = activate([outside(i, corners[i]), prev[:, r], prev[:, beyond]], order, sw, sb[...])
        mixed[:, place] = mix(before, hidden[i], latent[:, r], tw, tb[...])
    for k, out in zip(early, outs):
        out[...] = mixed[lax.bitwise_xor(me, k)]
    for k, out in zip(whole, outs[len(early) :]):
        frame = lax.bitwise_xor(me, k)
        out[0] = mixed[frame, 0]
        out[pl.ds(1, rows - 2)] = inner[frame]
        out[rows - 1] = mixed[frame, 1]


def grow_kernel(plan, pieces, out, grown, sems):
    tile = out.shape[1] // lax.axis_size("space")
    cols = out.shape[2] // 2
    me = lax.axis_index("space")
    at = lax.broadcasted_iota(jnp.int32, (2 * cols, cols), 0)
    of = lax.broadcasted_iota(jnp.int32, (2 * cols, cols), 1)
    twice = jnp.where(at // 2 == of, 1.0, 0.0).astype(BF16)
    copies, used = [], 0
    for (k, runs), piece in zip(plan, pieces):
        base, src = used, lax.bitwise_xor(me, k)
        for i in range(piece.shape[0]):
            wide = jnp.dot(twice, piece[i], preferred_element_type=jnp.float32).astype(BF16)
            grown[used] = wide
            grown[used + 1] = wide
            used += 2
        for first, rows in runs:
            copy = pltpu.make_async_copy(
                grown.at[pl.ds(base, 2 * rows)], out.at[0, pl.ds(src * tile + 2 * first, 2 * rows)], sems.at[len(copies)]
            )
            copy.start()
            copies.append(copy)
            base += 2 * rows
    for copy in copies:
        copy.wait()


def grow(plan, pieces, out, height, name):
    cols, chans = pieces[0].shape[1:]
    count = sum(p.shape[0] for p in pieces)
    extra = [] if out is None else [out]
    m = len(pieces)
    return pl.pallas_call(
        lambda *refs: grow_kernel(plan, refs[:m], *refs[m + len(extra) :]),
        out_shape=bf16(1, 2 * height, 2 * cols, chans),
        in_specs=[VMEM] * m + [HBM] * len(extra),
        out_specs=HBM,
        input_output_aliases={m: 0} if extra else {},
        scratch_shapes=[
            pltpu.VMEM((2 * count, 2 * cols, chans), BF16),
            pltpu.SemaphoreType.DMA((sum(len(runs) for _, runs in plan),)),
        ],
        compiler_params=PARAMS,
        cost_estimate=pl.CostEstimate(flops=0, transcendentals=0, bytes_accessed=8 * count * cols * chans),
        name=name,
    )(*pieces, *extra)


def cost(rows, taps, chans):
    return pl.CostEstimate(flops=2 * taps * rows * chans * chans, transcendentals=rows * chans, bytes_accessed=2 * MIB)


def swap(block, k):
    return lax.ppermute(block, "space", [(i, i ^ k) for i in range(lax.axis_size("space"))])


def ahead(block):
    n = lax.axis_size("tm")
    return lax.ppermute(block, "tm", [(t, (t + 1) % n) for t in range(n)])


def beside(block):
    n = lax.axis_size("space")
    route = [(s, (s + 1 if s % 2 else s - 1) % n) for s in range(n)]
    return lax.ppermute(block, "space", route)


def body(latent, spatial_weight, spatial_bias, temporal_weight, temporal_bias):
    frames, rows, cols, chans = latent.shape
    n = lax.axis_size("space")
    if n & (n - 1) or frames != n:
        raise ValueError("shape")
    early, whole = exchanges(n)

    args = [latent, spatial_weight, spatial_bias.reshape(1, chans), temporal_weight, temporal_bias.reshape(1, chans)]
    args = [pltpu.with_memory_space_constraint(a, pltpu.HBM) for a in args]
    near, far, last = pl.pallas_call(
        border_kernel,
        out_shape=[bf16(frames, cols, chans), bf16(frames, cols, chans), bf16(2, rows, cols, chans)],
        in_specs=[HBM],
        out_specs=[VMEM] * 3,
        scratch_shapes=[pltpu.SemaphoreType.DMA((3,))],
        compiler_params=PARAMS,
        name="border",
    )(args[0])
    near = swap(near, 1)
    far = beside(far)
    prev = ahead(last)
    latent, *params = pl.pallas_call(
        load_kernel,
        out_shape=[jax.ShapeDtypeStruct(a.shape, a.dtype) for a in args],
        in_specs=[HBM] * 5,
        out_specs=[VMEM] * 5,
        scratch_shapes=[pltpu.SemaphoreType.DMA((5,))],
        compiler_params=PARAMS,
        cost_estimate=pl.CostEstimate(flops=0, transcendentals=0, bytes_accessed=5 * MIB),
        name="load",
    )(*args)

    inner, *first = pl.pallas_call(
        lambda *refs: inner_kernel(early, *refs),
        out_shape=[bf16(frames, rows - 2, cols, chans)] + [bf16(rows - 2, cols, chans)] * len(early),
        in_specs=[VMEM] * 6,
        out_specs=[VMEM] * (1 + len(early)),
        compiler_params=PARAMS,
        cost_estimate=cost((frames + 2) * (rows - 2) * cols, 12, chans),
        name="inner",
    )(latent, prev, *params)
    first = [swap(piece, k) for k, piece in zip(early, first)]

    near, far, inner = lax.optimization_barrier((near, far, inner))
    corners = ahead(jnp.stack([near[frames - 2 :], far[frames - 2 :]]))
    hidden = pl.pallas_call(
        edge_kernel,
        out_shape=bf16(2, frames, cols, chans),
        in_specs=[VMEM] * 5,
        out_specs=VMEM,
        compiler_params=PARAMS,
        cost_estimate=cost(frames * 2 * cols, 9, chans),
        name="edge",
    )(latent, near, far, *params[:2])
    second = pl.pallas_call(
        lambda *refs: join_kernel(early, whole + [0], *refs),
        out_shape=[bf16(2, cols, chans)] * len(early) + [bf16(rows, cols, chans)] * (len(whole) + 1),
        in_specs=[VMEM] * 9,
        out_specs=[VMEM] * n,
        scratch_shapes=[pltpu.VMEM((frames, 2, cols, chans), BF16)],
        compiler_params=PARAMS,
        cost_estimate=cost(frames * 2 * cols, 6, chans),
        name="join",
    )(latent, prev, corners, hidden, inner, *params)
    own = second[-1]
    steps = early + whole
    sent = whole[: n // 2 - len(early)] + early + whole[n // 2 - len(early) :]
    second = {k: swap(second[steps.index(k)], k) for k in sent}

    out = grow([(k, [(1, rows - 2)]) for k in early] + [(0, [(0, rows)])], first + [own], None, rows * n, "grow_first")
    plan = [(k, [(0, 1), (rows - 1, 1)] if k in early else [(0, rows)]) for k in sent]
    return grow(plan, [second[k] for k in sent], out, rows * n, "grow_rest")


def solution(mesh):
    in_specs = (P("tm", "space", None, None), P(), P(), P(), P())
    out_specs = P(("tm", "space"), None, None, None)
    return jax.shard_map(body, mesh=mesh, in_specs=in_specs, out_specs=out_specs, check_vma=False)
```

```python
import jax
import jax.numpy as jnp
from jax import lax
from jax.experimental import pallas as pl
from jax.experimental.pallas import tpu as pltpu
from jax.sharding import PartitionSpec as P

VMEM = pl.BlockSpec(memory_space=pltpu.VMEM)
HBM = pl.BlockSpec(memory_space=pltpu.HBM)
ANY = pl.BlockSpec(memory_space=pl.ANY)
BF16 = jnp.bfloat16
MIB = 1 << 20
PARAMS = pltpu.CompilerParams(vmem_limit_bytes=24 * MIB)


def bf16(*shape):
    return jax.ShapeDtypeStruct(shape, BF16)


def exchanges(n):
    half = n // 2
    return list(range(1, half)) + sorted(range(half, n), key=lambda k: (k & 1, k))


def copy_all(pairs, sems):
    copies = [pltpu.make_async_copy(a, b, sems.at[i]) for i, (a, b) in enumerate(pairs)]
    for copy in copies:
        copy.start()
    for copy in copies:
        copy.wait()


def border_kernel(latent, near, far, last, sems):
    frames, rows = latent.shape[:2]
    odd = lax.rem(lax.axis_index("space"), 2)
    near_row, far_row = (rows - 1) * (1 - odd), (rows - 1) * odd
    pairs = [(latent.at[:, near_row], near), (latent.at[:, far_row], far), (latent.at[pl.ds(frames - 2, 2)], last)]
    copy_all(pairs, sems)


def load_kernel(*refs):
    m = len(refs) // 2
    copy_all(list(zip(refs[:m], refs[m : 2 * m])), refs[-1])


def activate(taps, order, weight_ref, bias):
    frames, cols, chans = taps[0].shape
    wide = jnp.concatenate([t.reshape(frames * cols, chans) for t in taps], axis=1)

    def tap(b):
        w = jnp.concatenate([weight_ref[a, b] for a in order], axis=0)
        return jnp.dot(wide, w, preferred_element_type=jnp.float32).reshape(frames, cols, chans)

    col = lax.broadcasted_iota(jnp.int32, (1, cols, chans), 1)
    left = jnp.where(col == 0, 0.0, pltpu.roll(tap(0), 1, axis=1))
    right = jnp.where(col == cols - 1, 0.0, pltpu.roll(tap(2), cols - 1, axis=1))
    half = 0.5 * (tap(1) + left + right + bias)
    return (half + half * jnp.tanh(half)).astype(BF16)


def mix(before, hidden, own, weight_ref, bias):
    frames, cols, chans = own.shape
    before = jnp.where(lax.axis_index("tm") > 0, before, jnp.zeros_like(before))
    joined = jnp.concatenate([before, hidden], axis=0)
    wide = jnp.concatenate([joined[k : k + frames].reshape(frames * cols, chans) for k in range(3)], axis=1)
    total = jnp.dot(wide, weight_ref[...].reshape(3 * chans, chans), preferred_element_type=jnp.float32)
    return (own.astype(jnp.float32) + total.reshape(frames, cols, chans) + bias).astype(BF16)


def inner_kernel(latent, sw, sb, hidden):
    for r in range(1, latent.shape[1] - 1):
        hidden[r - 1] = activate([latent[:, r + i] for i in (-1, 0, 1)], (0, 1, 2), sw, sb[...])


def inner_mix_kernel(latent, prev, hidden, sw, sb, tw, tb, out):
    for r in range(1, latent.shape[1] - 1):
        before = activate([prev[:, r + i] for i in (-1, 0, 1)], (0, 1, 2), sw, sb[...])
        out[:, r - 1] = mix(before, hidden[r - 1], latent[:, r], tw, tb[...])


def sides(rows):
    odd = lax.rem(lax.axis_index("space"), 2)
    for top in (odd, 1 - odd):
        yield (rows - 1) * (1 - top), 1 + (rows - 3) * (1 - top), 1 - top, (2 - 2 * top, 1, 2 * top)


def outside(i, halo):
    if i == 0:
        return halo
    me = lax.axis_index("space")
    inside = jnp.logical_and(me > 0, me < lax.axis_size("space") - 1)
    return jnp.where(inside, halo, jnp.zeros_like(halo))


def edge_kernel(latent, near, far, sw, sb, hidden):
    for i, (halo, (r, beyond, _, order)) in enumerate(zip((near, far), sides(latent.shape[1]))):
        hidden[i] = activate([outside(i, halo[...]), latent[:, r], latent[:, beyond]], order, sw, sb[...])


def join_kernel(steps, latent, prev, corners, hidden, sw, sb, tw_hbm, tb, *rest):
    outs, mixed, tw, sem = rest[:-3], *rest[-3:]
    copy = pltpu.make_async_copy(tw_hbm, tw, sem)
    copy.start()
    rows = latent.shape[1]
    me = lax.axis_index("space")
    before = [
        activate([outside(i, corners[i]), prev[:, r], prev[:, beyond]], order, sw, sb[...])
        for i, (r, beyond, _, order) in enumerate(sides(rows))
    ]
    copy.wait()
    for i, (r, _, place, _) in enumerate(sides(rows)):
        mixed[:, place] = mix(before[i], hidden[i], latent[:, r], tw, tb[...])
    for k, out in zip(steps, outs):
        out[...] = mixed[lax.bitwise_xor(me, k)]


def grow_kernel(plan, pieces, out, grown, sems):
    tile = out.shape[1] // lax.axis_size("space")
    cols = out.shape[2] // 2
    me = lax.axis_index("space")
    at = lax.broadcasted_iota(jnp.int32, (2 * cols, cols), 0)
    of = lax.broadcasted_iota(jnp.int32, (2 * cols, cols), 1)
    twice = jnp.where(at // 2 == of, 1.0, 0.0).astype(BF16)
    rows = [(piece, i) for piece in pieces for i in range(piece.shape[0])]
    copies, used = [], 0
    for src, k, runs in plan:
        src = lax.bitwise_xor(me, k) if src is None else src
        for first, count in runs:
            for i in range(count):
                piece, r = rows[used + i]
                wide = jnp.dot(twice, piece[r], preferred_element_type=jnp.float32).astype(BF16)
                grown[2 * (used + i)] = wide
                grown[2 * (used + i) + 1] = wide
            copy = pltpu.make_async_copy(
                grown.at[pl.ds(2 * used, 2 * count)],
                out.at[0, pl.ds(src * tile + 2 * first, 2 * count)],
                sems.at[len(copies)],
            )
            copy.start()
            copies.append(copy)
            used += count
    for copy in copies:
        copy.wait()


def grow(plan, pieces, out, height, name):
    cols, chans = pieces[0].shape[1:]
    count = sum(p.shape[0] for p in pieces)
    extra = [] if out is None else [out]
    m = len(pieces)
    return pl.pallas_call(
        lambda *refs: grow_kernel(plan, refs[:m], *refs[m + len(extra) :]),
        out_shape=bf16(1, 2 * height, 2 * cols, chans),
        in_specs=[VMEM] * m + [HBM] * len(extra),
        out_specs=HBM,
        input_output_aliases={m: 0} if extra else {},
        scratch_shapes=[
            pltpu.VMEM((2 * count, 2 * cols, chans), BF16),
            pltpu.SemaphoreType.DMA((sum(len(runs) for _, _, runs in plan),)),
        ],
        compiler_params=PARAMS,
        cost_estimate=pl.CostEstimate(flops=0, transcendentals=0, bytes_accessed=8 * count * cols * chans),
        name=name,
    )(*pieces, *extra)


def cost(rows, taps, chans):
    return pl.CostEstimate(flops=2 * taps * rows * chans * chans, transcendentals=rows * chans, bytes_accessed=2 * MIB)


def swap(block, k):
    return lax.ppermute(block, "space", [(i, i ^ k) for i in range(lax.axis_size("space"))])


def ahead(block):
    n = lax.axis_size("tm")
    return lax.ppermute(block, "tm", [(t, (t + 1) % n) for t in range(n)])


def beside(block):
    n = lax.axis_size("space")
    route = [(s, (s + 1 if s % 2 else s - 1) % n) for s in range(n)]
    return lax.ppermute(block, "space", route)


def body(latent, spatial_weight, spatial_bias, temporal_weight, temporal_bias):
    frames, rows, cols, chans = latent.shape
    n = lax.axis_size("space")
    if n & (n - 1) or frames != n:
        raise ValueError("shape")
    steps = exchanges(n)

    args = [latent, spatial_weight, spatial_bias.reshape(1, chans), temporal_weight, temporal_bias.reshape(1, chans)]
    args = [pltpu.with_memory_space_constraint(a, pltpu.HBM) for a in args]
    near, far, last = pl.pallas_call(
        border_kernel,
        out_shape=[bf16(frames, cols, chans), bf16(frames, cols, chans), bf16(2, rows, cols, chans)],
        in_specs=[HBM],
        out_specs=[VMEM] * 3,
        scratch_shapes=[pltpu.SemaphoreType.DMA((3,))],
        compiler_params=PARAMS,
        name="border",
    )(args[0])
    near = swap(near, 1)
    far = beside(far)
    prev = ahead(last)
    latent, *params = pl.pallas_call(
        load_kernel,
        out_shape=[jax.ShapeDtypeStruct(a.shape, a.dtype) for a in args],
        in_specs=[HBM] * 5,
        out_specs=[VMEM] * 5,
        scratch_shapes=[pltpu.SemaphoreType.DMA((5,))],
        compiler_params=PARAMS,
        cost_estimate=pl.CostEstimate(flops=0, transcendentals=0, bytes_accessed=5 * MIB),
        name="load",
    )(*args)

    hidden = pl.pallas_call(
        inner_kernel,
        out_shape=bf16(rows - 2, frames, cols, chans),
        in_specs=[VMEM] * 3,
        out_specs=VMEM,
        compiler_params=PARAMS,
        cost_estimate=cost(frames * (rows - 2) * cols, 9, chans),
        name="inner",
    )(latent, *params[:2])
    inner = pl.pallas_call(
        inner_mix_kernel,
        out_shape=bf16(frames, rows - 2, cols, chans),
        in_specs=[VMEM] * 7,
        out_specs=VMEM,
        compiler_params=PARAMS,
        cost_estimate=cost(frames * (rows - 2) * cols, 6, chans),
        name="inner_mix",
    )(latent, prev, hidden, *params)
    inner_own = inner
    inner = lax.all_to_all(inner, "space", split_axis=0, concat_axis=1, tiled=True)[0]

    near, far, token = lax.optimization_barrier((near, far, inner_own))
    corners = ahead(jnp.stack([near[frames - 2 :], far[frames - 2 :]]))
    hidden = pl.pallas_call(
        edge_kernel,
        out_shape=bf16(2, frames, cols, chans),
        in_specs=[VMEM] * 5,
        out_specs=VMEM,
        compiler_params=PARAMS,
        cost_estimate=cost(frames * 2 * cols, 9, chans),
        name="edge",
    )(latent, near, far, *params[:2])
    edges = pl.pallas_call(
        lambda *refs: join_kernel([0] + steps, *refs),
        out_shape=[bf16(2, cols, chans)] * n,
        in_specs=[VMEM] * 6 + [HBM, VMEM],
        out_specs=[VMEM] * n,
        scratch_shapes=[
            pltpu.VMEM((frames, 2, cols, chans), BF16),
            pltpu.VMEM(temporal_weight.shape, BF16),
            pltpu.SemaphoreType.DMA,
        ],
        compiler_params=PARAMS,
        cost_estimate=cost(frames * 2 * cols, 6, chans),
        name="join",
    )(latent, prev, corners, hidden, *params[:2], args[3], params[3])
    edges = [edges[0]] + [swap(edge, k) for k, edge in zip(steps, edges[1:])]

    out = grow([(s, None, [(1, rows - 2)]) for s in range(n)], [pltpu.with_memory_space_constraint(inner, pltpu.HBM)], None, rows * n, "grow_inner")
    ends = [(0, 1), (rows - 1, 1)]
    out = grow([(None, k, ends) for k in [0] + steps[:n // 2]], edges[: n // 2 + 1], out, rows * n, "grow_first")
    return grow([(None, k, ends) for k in steps[n // 2:]], edges[n // 2 + 1 :], out, rows * n, "grow_last")


def solution(mesh):
    in_specs = (P("tm", "space", None, None), P(), P(), P(), P())
    out_specs = P(("tm", "space"), None, None, None)
    return jax.shard_map(body, mesh=mesh, in_specs=in_specs, out_specs=out_specs, check_vma=False)
```

```python
import jax
import jax.numpy as jnp
from jax import lax
from jax.experimental import pallas as pl
from jax.experimental.pallas import tpu as pltpu
from jax.sharding import PartitionSpec as P

VMEM = pl.BlockSpec(memory_space=pltpu.VMEM)
HBM = pl.BlockSpec(memory_space=pltpu.HBM)
ANY = pl.BlockSpec(memory_space=pl.ANY)
BF16 = jnp.bfloat16
MIB = 1 << 20
PARAMS = pltpu.CompilerParams(vmem_limit_bytes=24 * MIB)


def bf16(*shape):
    return jax.ShapeDtypeStruct(shape, BF16)


def exchanges(n):
    half = n // 2
    return list(range(2, half)) + sorted(range(half, n), key=lambda k: (k & 1, k)) + [1]


def copy_all(pairs, sems):
    copies = [pltpu.make_async_copy(a, b, sems.at[i]) for i, (a, b) in enumerate(pairs)]
    for copy in copies:
        copy.start()
    for copy in copies:
        copy.wait()


def border_kernel(latent, near, far, last, sems):
    frames, rows = latent.shape[:2]
    odd = lax.rem(lax.axis_index("space"), 2)
    near_row, far_row = (rows - 1) * (1 - odd), (rows - 1) * odd
    pairs = [(latent.at[:, near_row], near), (latent.at[:, far_row], far), (latent.at[pl.ds(frames - 2, 2)], last)]
    copy_all(pairs, sems)


def load_kernel(*refs):
    m = len(refs) // 2
    copy_all(list(zip(refs[:m], refs[m : 2 * m])), refs[-1])


def activate(taps, order, weight_ref, bias):
    frames, cols, chans = taps[0].shape
    wide = jnp.concatenate([t.reshape(frames * cols, chans) for t in taps], axis=1)

    def tap(b):
        w = jnp.concatenate([weight_ref[a, b] for a in order], axis=0)
        return jnp.dot(wide, w, preferred_element_type=jnp.float32).reshape(frames, cols, chans)

    col = lax.broadcasted_iota(jnp.int32, (1, cols, chans), 1)
    left = jnp.where(col == 0, 0.0, pltpu.roll(tap(0), 1, axis=1))
    right = jnp.where(col == cols - 1, 0.0, pltpu.roll(tap(2), cols - 1, axis=1))
    half = 0.5 * (tap(1) + left + right + bias)
    return (half + half * jnp.tanh(half)).astype(BF16)


def mix(before, hidden, own, weight_ref, bias):
    frames, cols, chans = own.shape
    before = jnp.where(lax.axis_index("tm") > 0, before, jnp.zeros_like(before))
    joined = jnp.concatenate([before, hidden], axis=0)
    wide = jnp.concatenate([joined[k : k + frames].reshape(frames * cols, chans) for k in range(3)], axis=1)
    total = jnp.dot(wide, weight_ref[...].reshape(3 * chans, chans), preferred_element_type=jnp.float32)
    return (own.astype(jnp.float32) + total.reshape(frames, cols, chans) + bias).astype(BF16)


def inner_kernel(latent, sw, sb, hidden):
    for r in range(1, latent.shape[1] - 1):
        hidden[r - 1] = activate([latent[:, r + i] for i in (-1, 0, 1)], (0, 1, 2), sw, sb[...])


def inner_mix_kernel(latent, prev, hidden, sw, sb, tw, tb, out):
    for r in range(1, latent.shape[1] - 1):
        before = activate([prev[:, r + i] for i in (-1, 0, 1)], (0, 1, 2), sw, sb[...])
        out[:, r - 1] = mix(before, hidden[r - 1], latent[:, r], tw, tb[...])


def sides(rows):
    odd = lax.rem(lax.axis_index("space"), 2)
    for top in (odd, 1 - odd):
        yield (rows - 1) * (1 - top), 1 + (rows - 3) * (1 - top), 1 - top, (2 - 2 * top, 1, 2 * top)


def outside(i, halo):
    if i == 0:
        return halo
    me = lax.axis_index("space")
    inside = jnp.logical_and(me > 0, me < lax.axis_size("space") - 1)
    return jnp.where(inside, halo, jnp.zeros_like(halo))


def edge_kernel(latent, near, far, sw, sb, tw, hidden, tw_v, sem):
    copy = pltpu.make_async_copy(tw, tw_v, sem)
    copy.start()
    for i, (halo, (r, beyond, _, order)) in enumerate(zip((near, far), sides(latent.shape[1]))):
        hidden[i] = activate([outside(i, halo[...]), latent[:, r], latent[:, beyond]], order, sw, sb[...])
    copy.wait()


def join_kernel(steps, latent, prev, corners, hidden, sw, sb, tw, tb, *rest):
    outs, mixed = rest[:-1], rest[-1]
    rows = latent.shape[1]
    me = lax.axis_index("space")
    before = [
        activate([outside(i, corners[i]), prev[:, r], prev[:, beyond]], order, sw, sb[...])
        for i, (r, beyond, _, order) in enumerate(sides(rows))
    ]
    for i, (r, _, place, _) in enumerate(sides(rows)):
        mixed[:, place] = mix(before[i], hidden[i], latent[:, r], tw, tb[...])
    for k, out in zip(steps, outs):
        out[...] = mixed[lax.bitwise_xor(me, k)]


def grow_kernel(plan, pieces, out, grown, sems):
    tile = out.shape[1] // lax.axis_size("space")
    cols = out.shape[2] // 2
    me = lax.axis_index("space")
    at = lax.broadcasted_iota(jnp.int32, (2 * cols, cols), 0)
    of = lax.broadcasted_iota(jnp.int32, (2 * cols, cols), 1)
    twice = jnp.where(at // 2 == of, 1.0, 0.0).astype(BF16)
    rows = [(piece, i) for piece in pieces for i in range(piece.shape[0])]
    copies, used = [], 0
    for src, k, runs in plan:
        src = lax.bitwise_xor(me, k) if src is None else src
        for first, count in runs:
            for i in range(count):
                piece, r = rows[used + i]
                wide = jnp.dot(twice, piece[r], preferred_element_type=jnp.float32).astype(BF16)
                grown[2 * (used + i)] = wide
                grown[2 * (used + i) + 1] = wide
            copy = pltpu.make_async_copy(
                grown.at[pl.ds(2 * used, 2 * count)],
                out.at[0, pl.ds(src * tile + 2 * first, 2 * count)],
                sems.at[len(copies)],
            )
            copy.start()
            copies.append(copy)
            used += count
    for copy in copies:
        copy.wait()


def grow(plan, pieces, out, height, name):
    cols, chans = pieces[0].shape[1:]
    count = sum(p.shape[0] for p in pieces)
    extra = [] if out is None else [out]
    m = len(pieces)
    return pl.pallas_call(
        lambda *refs: grow_kernel(plan, refs[:m], *refs[m + len(extra) :]),
        out_shape=bf16(1, 2 * height, 2 * cols, chans),
        in_specs=[VMEM] * m + [HBM] * len(extra),
        out_specs=HBM,
        input_output_aliases={m: 0} if extra else {},
        scratch_shapes=[
            pltpu.VMEM((2 * count, 2 * cols, chans), BF16),
            pltpu.SemaphoreType.DMA((sum(len(runs) for _, _, runs in plan),)),
        ],
        compiler_params=PARAMS,
        cost_estimate=pl.CostEstimate(flops=0, transcendentals=0, bytes_accessed=8 * count * cols * chans),
        name=name,
    )(*pieces, *extra)


def cost(rows, taps, chans):
    return pl.CostEstimate(flops=2 * taps * rows * chans * chans, transcendentals=rows * chans, bytes_accessed=2 * MIB)


def swap(block, k):
    return lax.ppermute(block, "space", [(i, i ^ k) for i in range(lax.axis_size("space"))])


def ahead(block):
    n = lax.axis_size("tm")
    return lax.ppermute(block, "tm", [(t, (t + 1) % n) for t in range(n)])


def beside(block):
    ts, n = lax.axis_size("tm"), lax.axis_size("space")
    route = []
    for t in range(ts):
        for s in range(n):
            to = (t ^ 1 if t ^ 1 < ts else t, s) if s in (0, n - 1) else (t, s + 1 if s % 2 else s - 1)
            route.append((t * n + s, to[0] * n + to[1]))
    return lax.ppermute(block, ("tm", "space"), route)


def body(latent, spatial_weight, spatial_bias, temporal_weight, temporal_bias):
    frames, rows, cols, chans = latent.shape
    n = lax.axis_size("space")
    if n & (n - 1) or frames != n:
        raise ValueError("shape")
    steps = exchanges(n)

    args = [latent, spatial_weight, spatial_bias.reshape(1, chans), temporal_weight, temporal_bias.reshape(1, chans)]
    args = [pltpu.with_memory_space_constraint(a, pltpu.HBM) for a in args]
    near, far, last = pl.pallas_call(
        border_kernel,
        out_shape=[bf16(frames, cols, chans), bf16(frames, cols, chans), bf16(2, rows, cols, chans)],
        in_specs=[HBM],
        out_specs=[VMEM] * 3,
        scratch_shapes=[pltpu.SemaphoreType.DMA((3,))],
        compiler_params=PARAMS,
        name="border",
    )(args[0])
    near = swap(near, 1)
    far = beside(far)
    prev = ahead(last)
    latent, *params = pl.pallas_call(
        load_kernel,
        out_shape=[jax.ShapeDtypeStruct(a.shape, a.dtype) for a in args],
        in_specs=[HBM] * 5,
        out_specs=[VMEM] * 5,
        scratch_shapes=[pltpu.SemaphoreType.DMA((5,))],
        compiler_params=PARAMS,
        cost_estimate=pl.CostEstimate(flops=0, transcendentals=0, bytes_accessed=5 * MIB),
        name="load",
    )(*args)

    hidden = pl.pallas_call(
        inner_kernel,
        out_shape=bf16(rows - 2, frames, cols, chans),
        in_specs=[VMEM] * 3,
        out_specs=VMEM,
        compiler_params=PARAMS,
        cost_estimate=cost(frames * (rows - 2) * cols, 9, chans),
        name="inner",
    )(latent, *params[:2])
    inner = pl.pallas_call(
        inner_mix_kernel,
        out_shape=bf16(frames, rows - 2, cols, chans),
        in_specs=[VMEM] * 7,
        out_specs=VMEM,
        compiler_params=PARAMS,
        cost_estimate=cost(frames * (rows - 2) * cols, 6, chans),
        name="inner_mix",
    )(latent, prev, hidden, *params)
    inner_own = inner
    inner = lax.all_to_all(inner, "space", split_axis=0, concat_axis=1, tiled=True)[0]

    near, far, token = lax.optimization_barrier((near, far, inner_own))
    corners = ahead(jnp.stack([near[frames - 2 :], far[frames - 2 :]]))
    hidden, tw = pl.pallas_call(
        edge_kernel,
        out_shape=[bf16(2, frames, cols, chans), bf16(*temporal_weight.shape)],
        in_specs=[VMEM] * 5 + [HBM],
        out_specs=[VMEM] * 2,
        scratch_shapes=[pltpu.SemaphoreType.DMA],
        compiler_params=PARAMS,
        cost_estimate=cost(frames * 2 * cols, 9, chans),
        name="edge",
    )(latent, near, far, *params[:2], args[3])
    edges = pl.pallas_call(
        lambda *refs: join_kernel([0] + steps, *refs),
        out_shape=[bf16(2, cols, chans)] * n,
        in_specs=[VMEM] * 8,
        out_specs=[VMEM] * n,
        scratch_shapes=[pltpu.VMEM((frames, 2, cols, chans), BF16)],
        compiler_params=PARAMS,
        cost_estimate=cost(frames * 2 * cols, 6, chans),
        name="join",
    )(latent, prev, corners, hidden, *params[:2], tw, params[3])
    edges = [edges[0]] + [swap(edge, k) for k, edge in zip(steps, edges[1:])]

    out = grow([(s, None, [(1, rows - 2)]) for s in range(n)], [pltpu.with_memory_space_constraint(inner, pltpu.HBM)], None, rows * n, "grow_inner")
    ends = [(0, 1), (rows - 1, 1)]
    out = grow([(None, k, ends) for k in [0] + steps[:n // 2]], edges[: n // 2 + 1], out, rows * n, "grow_first")
    return grow([(None, k, ends) for k in steps[n // 2:]], edges[n // 2 + 1 :], out, rows * n, "grow_last")


def solution(mesh):
    in_specs = (P("tm", "space", None, None), P(), P(), P(), P())
    out_specs = P(("tm", "space"), None, None, None)
    return jax.shard_map(body, mesh=mesh, in_specs=in_specs, out_specs=out_specs, check_vma=False)
```

```python
import jax
import jax.numpy as jnp
from jax import lax
from jax.experimental import pallas as pl
from jax.experimental.pallas import tpu as pltpu
from jax.sharding import PartitionSpec as P

VMEM = pl.BlockSpec(memory_space=pltpu.VMEM)
HBM = pl.BlockSpec(memory_space=pltpu.HBM)
ANY = pl.BlockSpec(memory_space=pl.ANY)
BF16 = jnp.bfloat16
MIB = 1 << 20
PARAMS = pltpu.CompilerParams(vmem_limit_bytes=24 * MIB)


def bf16(*shape):
    return jax.ShapeDtypeStruct(shape, BF16)


def exchanges(n):
    half = n // 2
    return list(range(2, half)) + [k ^ 1 for k in range(half, n)] + [1]


def copy_all(pairs, sems):
    copies = [pltpu.make_async_copy(a, b, sems.at[i]) for i, (a, b) in enumerate(pairs)]
    for copy in copies:
        copy.start()
    for copy in copies:
        copy.wait()


def border_kernel(latent, near, far, last, sems):
    frames, rows = latent.shape[:2]
    odd = lax.rem(lax.axis_index("space"), 2)
    near_row, far_row = (rows - 1) * (1 - odd), (rows - 1) * odd
    pairs = [(latent.at[:, near_row], near), (latent.at[:, far_row], far), (latent.at[pl.ds(frames - 2, 2)], last)]
    copy_all(pairs, sems)


def load_kernel(*refs):
    m = len(refs) // 2
    copy_all(list(zip(refs[:m], refs[m : 2 * m])), refs[-1])


def activate(taps, order, weight_ref, bias):
    frames, cols, chans = taps[0].shape
    wide = jnp.concatenate([t.reshape(frames * cols, chans) for t in taps], axis=1)

    def tap(b):
        w = jnp.concatenate([weight_ref[a, b] for a in order], axis=0)
        return jnp.dot(wide, w, preferred_element_type=jnp.float32).reshape(frames, cols, chans)

    col = lax.broadcasted_iota(jnp.int32, (1, cols, chans), 1)
    left = jnp.where(col == 0, 0.0, pltpu.roll(tap(0), 1, axis=1))
    right = jnp.where(col == cols - 1, 0.0, pltpu.roll(tap(2), cols - 1, axis=1))
    half = 0.5 * (tap(1) + left + right + bias)
    return (half + half * jnp.tanh(half)).astype(BF16)


def mix(before, hidden, own, weight_ref, bias):
    frames, cols, chans = own.shape
    before = jnp.where(lax.axis_index("tm") > 0, before, jnp.zeros_like(before))
    joined = jnp.concatenate([before, hidden], axis=0)
    wide = jnp.concatenate([joined[k : k + frames].reshape(frames * cols, chans) for k in range(3)], axis=1)
    total = jnp.dot(wide, weight_ref[...].reshape(3 * chans, chans), preferred_element_type=jnp.float32)
    return (own.astype(jnp.float32) + total.reshape(frames, cols, chans) + bias).astype(BF16)


def inner_kernel(latent, sw, sb, hidden):
    for r in range(1, latent.shape[1] - 1):
        hidden[r - 1] = activate([latent[:, r + i] for i in (-1, 0, 1)], (0, 1, 2), sw, sb[...])


def inner_mix_kernel(latent, prev, hidden, sw, sb, tw, tb, out):
    for r in range(1, latent.shape[1] - 1):
        before = activate([prev[:, r + i] for i in (-1, 0, 1)], (0, 1, 2), sw, sb[...])
        out[:, r - 1] = mix(before, hidden[r - 1], latent[:, r], tw, tb[...])


def sides(rows):
    odd = lax.rem(lax.axis_index("space"), 2)
    for top in (odd, 1 - odd):
        yield (rows - 1) * (1 - top), 1 + (rows - 3) * (1 - top), 1 - top, (2 - 2 * top, 1, 2 * top)


def outside(i, halo):
    if i == 0:
        return halo
    me = lax.axis_index("space")
    inside = jnp.logical_and(me > 0, me < lax.axis_size("space") - 1)
    return jnp.where(inside, halo, jnp.zeros_like(halo))


def edge_kernel(latent, near, far, sw, sb, tw, hidden, tw_v, sem):
    copy = pltpu.make_async_copy(tw, tw_v, sem)
    copy.start()
    for i, (halo, (r, beyond, _, order)) in enumerate(zip((near, far), sides(latent.shape[1]))):
        hidden[i] = activate([outside(i, halo[...]), latent[:, r], latent[:, beyond]], order, sw, sb[...])
    copy.wait()


def join_kernel(steps, latent, prev, corners, hidden, sw, sb, tw, tb, *rest):
    outs, mixed = rest[:-1], rest[-1]
    rows = latent.shape[1]
    me = lax.axis_index("space")
    before = [
        activate([outside(i, corners[i]), prev[:, r], prev[:, beyond]], order, sw, sb[...])
        for i, (r, beyond, _, order) in enumerate(sides(rows))
    ]
    for i, (r, _, place, _) in enumerate(sides(rows)):
        mixed[:, place] = mix(before[i], hidden[i], latent[:, r], tw, tb[...])
    for k, out in zip(steps, outs):
        out[...] = mixed[lax.bitwise_xor(me, k)]


def grow_kernel(plan, pieces, out, grown, sems):
    tile = out.shape[1] // lax.axis_size("space")
    cols = out.shape[2] // 2
    me = lax.axis_index("space")
    at = lax.broadcasted_iota(jnp.int32, (2 * cols, cols), 0)
    of = lax.broadcasted_iota(jnp.int32, (2 * cols, cols), 1)
    twice = jnp.where(at // 2 == of, 1.0, 0.0).astype(BF16)
    rows = [(piece, i) for piece in pieces for i in range(piece.shape[0])]
    copies, used = [], 0
    for src, k, runs in plan:
        src = lax.bitwise_xor(me, k) if src is None else src
        for first, count in runs:
            for i in range(count):
                piece, r = rows[used + i]
                wide = jnp.dot(twice, piece[r], preferred_element_type=jnp.float32).astype(BF16)
                grown[2 * (used + i)] = wide
                grown[2 * (used + i) + 1] = wide
            copy = pltpu.make_async_copy(
                grown.at[pl.ds(2 * used, 2 * count)],
                out.at[0, pl.ds(src * tile + 2 * first, 2 * count)],
                sems.at[len(copies)],
            )
            copy.start()
            copies.append(copy)
            used += count
    for copy in copies:
        copy.wait()


def grow(plan, pieces, out, height, name):
    cols, chans = pieces[0].shape[1:]
    count = sum(p.shape[0] for p in pieces)
    extra = [] if out is None else [out]
    m = len(pieces)
    return pl.pallas_call(
        lambda *refs: grow_kernel(plan, refs[:m], *refs[m + len(extra) :]),
        out_shape=bf16(1, 2 * height, 2 * cols, chans),
        in_specs=[VMEM] * m + [HBM] * len(extra),
        out_specs=HBM,
        input_output_aliases={m: 0} if extra else {},
        scratch_shapes=[
            pltpu.VMEM((2 * count, 2 * cols, chans), BF16),
            pltpu.SemaphoreType.DMA((sum(len(runs) for _, _, runs in plan),)),
        ],
        compiler_params=PARAMS,
        cost_estimate=pl.CostEstimate(flops=0, transcendentals=0, bytes_accessed=8 * count * cols * chans),
        name=name,
    )(*pieces, *extra)


def cost(rows, taps, chans):
    return pl.CostEstimate(flops=2 * taps * rows * chans * chans, transcendentals=rows * chans, bytes_accessed=2 * MIB)


def swap(block, k):
    return lax.ppermute(block, "space", [(i, i ^ k) for i in range(lax.axis_size("space"))])


def ahead(block):
    n = lax.axis_size("tm")
    return lax.ppermute(block, "tm", [(t, (t + 1) % n) for t in range(n)])


def beside(block):
    ts, n = lax.axis_size("tm"), lax.axis_size("space")
    route = []
    for t in range(ts):
        for s in range(n):
            to = (t ^ 1 if t ^ 1 < ts else t, s) if s in (0, n - 1) else (t, s + 1 if s % 2 else s - 1)
            route.append((t * n + s, to[0] * n + to[1]))
    return lax.ppermute(block, ("tm", "space"), route)


def body(latent, spatial_weight, spatial_bias, temporal_weight, temporal_bias):
    frames, rows, cols, chans = latent.shape
    n = lax.axis_size("space")
    if n & (n - 1) or frames != n:
        raise ValueError("shape")
    steps = exchanges(n)

    args = [latent, spatial_weight, spatial_bias.reshape(1, chans), temporal_weight, temporal_bias.reshape(1, chans)]
    args = [pltpu.with_memory_space_constraint(a, pltpu.HBM) for a in args]
    near, far, last = pl.pallas_call(
        border_kernel,
        out_shape=[bf16(frames, cols, chans), bf16(frames, cols, chans), bf16(2, rows, cols, chans)],
        in_specs=[HBM],
        out_specs=[VMEM] * 3,
        scratch_shapes=[pltpu.SemaphoreType.DMA((3,))],
        compiler_params=PARAMS,
        name="border",
    )(args[0])
    near = swap(near, 1)
    far = beside(far)
    prev = ahead(last)
    latent, *params = pl.pallas_call(
        load_kernel,
        out_shape=[jax.ShapeDtypeStruct(a.shape, a.dtype) for a in args],
        in_specs=[HBM] * 5,
        out_specs=[VMEM] * 5,
        scratch_shapes=[pltpu.SemaphoreType.DMA((5,))],
        compiler_params=PARAMS,
        cost_estimate=pl.CostEstimate(flops=0, transcendentals=0, bytes_accessed=5 * MIB),
        name="load",
    )(*args)

    hidden = pl.pallas_call(
        inner_kernel,
        out_shape=bf16(rows - 2, frames, cols, chans),
        in_specs=[VMEM] * 3,
        out_specs=VMEM,
        compiler_params=PARAMS,
        cost_estimate=cost(frames * (rows - 2) * cols, 9, chans),
        name="inner",
    )(latent, *params[:2])
    inner = pl.pallas_call(
        inner_mix_kernel,
        out_shape=bf16(frames, rows - 2, cols, chans),
        in_specs=[VMEM] * 7,
        out_specs=VMEM,
        compiler_params=PARAMS,
        cost_estimate=cost(frames * (rows - 2) * cols, 6, chans),
        name="inner_mix",
    )(latent, prev, hidden, *params)
    inner_own = inner
    inner = lax.all_to_all(inner, "space", split_axis=0, concat_axis=1, tiled=True)[0]

    near, far, token = lax.optimization_barrier((near, far, inner_own))
    corners = ahead(jnp.stack([near[frames - 2 :], far[frames - 2 :]]))
    hidden, tw = pl.pallas_call(
        edge_kernel,
        out_shape=[bf16(2, frames, cols, chans), bf16(*temporal_weight.shape)],
        in_specs=[VMEM] * 5 + [HBM],
        out_specs=[VMEM] * 2,
        scratch_shapes=[pltpu.SemaphoreType.DMA],
        compiler_params=PARAMS,
        cost_estimate=cost(frames * 2 * cols, 9, chans),
        name="edge",
    )(latent, near, far, *params[:2], args[3])
    edges = pl.pallas_call(
        lambda *refs: join_kernel([0] + steps, *refs),
        out_shape=[bf16(2, cols, chans)] * n,
        in_specs=[VMEM] * 8,
        out_specs=[VMEM] * n,
        scratch_shapes=[pltpu.VMEM((frames, 2, cols, chans), BF16)],
        compiler_params=PARAMS,
        cost_estimate=cost(frames * 2 * cols, 6, chans),
        name="join",
    )(latent, prev, corners, hidden, *params[:2], tw, params[3])
    edges = [edges[0]] + [swap(edge, k) for k, edge in zip(steps, edges[1:])]

    out = grow([(s, None, [(1, rows - 2)]) for s in range(n)], [pltpu.with_memory_space_constraint(inner, pltpu.HBM)], None, rows * n, "grow_inner")
    ends = [(0, 1), (rows - 1, 1)]
    cut = 2
    out = grow([(None, k, ends) for k in [0] + steps[:cut]], edges[: cut + 1], out, rows * n, "grow_first")
    return grow([(None, k, ends) for k in steps[cut:]], edges[cut + 1 :], out, rows * n, "grow_last")


def solution(mesh):
    in_specs = (P("tm", "space", None, None), P(), P(), P(), P())
    out_specs = P(("tm", "space"), None, None, None)
    return jax.shard_map(body, mesh=mesh, in_specs=in_specs, out_specs=out_specs, check_vma=False)
```

```python
import jax
import jax.numpy as jnp
from jax import lax
from jax.experimental import pallas as pl
from jax.experimental.pallas import tpu as pltpu
from jax.sharding import PartitionSpec as P

VMEM = pl.BlockSpec(memory_space=pltpu.VMEM)
HBM = pl.BlockSpec(memory_space=pltpu.HBM)
ANY = pl.BlockSpec(memory_space=pl.ANY)
BF16 = jnp.bfloat16
MIB = 1 << 20
PARAMS = pltpu.CompilerParams(vmem_limit_bytes=24 * MIB)


def bf16(*shape):
    return jax.ShapeDtypeStruct(shape, BF16)


def exchanges(n):
    half = n // 2
    return list(range(2, half)) + [k ^ 1 for k in range(half, n)] + [1]


def copy_all(pairs, sems):
    copies = [pltpu.make_async_copy(a, b, sems.at[i]) for i, (a, b) in enumerate(pairs)]
    for copy in copies:
        copy.start()
    for copy in copies:
        copy.wait()


def border_kernel(latent, near, far, last, sems):
    frames, rows = latent.shape[:2]
    odd = lax.rem(lax.axis_index("space"), 2)
    near_row, far_row = (rows - 1) * (1 - odd), (rows - 1) * odd
    pairs = [(latent.at[:, near_row], near), (latent.at[:, far_row], far), (latent.at[pl.ds(frames - 2, 2)], last)]
    copy_all(pairs, sems)


def activate(taps, order, weight_ref, bias):
    frames, cols, chans = taps[0].shape
    wide = jnp.concatenate([t.reshape(frames * cols, chans) for t in taps], axis=1)

    def tap(b):
        w = jnp.concatenate([weight_ref[a, b] for a in order], axis=0)
        return jnp.dot(wide, w, preferred_element_type=jnp.float32).reshape(frames, cols, chans)

    col = lax.broadcasted_iota(jnp.int32, (1, cols, chans), 1)
    left = jnp.where(col == 0, 0.0, pltpu.roll(tap(0), 1, axis=1))
    right = jnp.where(col == cols - 1, 0.0, pltpu.roll(tap(2), cols - 1, axis=1))
    half = 0.5 * (tap(1) + left + right + bias)
    return (half + half * jnp.tanh(half)).astype(BF16)


def mix(before, hidden, own, weight_ref, bias):
    frames, cols, chans = own.shape
    before = jnp.where(lax.axis_index("tm") > 0, before, jnp.zeros_like(before))
    joined = jnp.concatenate([before, hidden], axis=0)
    wide = jnp.concatenate([joined[k : k + frames].reshape(frames * cols, chans) for k in range(3)], axis=1)
    total = jnp.dot(wide, weight_ref[...].reshape(3 * chans, chans), preferred_element_type=jnp.float32)
    return (own.astype(jnp.float32) + total.reshape(frames, cols, chans) + bias).astype(BF16)


def inner_kernel(*refs):
    args, (hidden, *loaded), sems = refs[:5], refs[5:11], refs[11]
    copies = [pltpu.make_async_copy(a, b, sems.at[i]) for i, (a, b) in enumerate(zip(args, loaded))]
    for copy in copies:
        copy.start()
    latent, sw, sb = loaded[:3]
    for copy in copies[:3]:
        copy.wait()
    for r in range(1, latent.shape[1] - 1):
        hidden[r - 1] = activate([latent[:, r + i] for i in (-1, 0, 1)], (0, 1, 2), sw, sb[...])
    for copy in copies[3:]:
        copy.wait()


def inner_mix_kernel(latent, prev, hidden, sw, sb, tw, tb, out):
    for r in range(1, latent.shape[1] - 1):
        before = activate([prev[:, r + i] for i in (-1, 0, 1)], (0, 1, 2), sw, sb[...])
        out[:, r - 1] = mix(before, hidden[r - 1], latent[:, r], tw, tb[...])


def sides(rows):
    odd = lax.rem(lax.axis_index("space"), 2)
    for top in (odd, 1 - odd):
        yield (rows - 1) * (1 - top), 1 + (rows - 3) * (1 - top), 1 - top, (2 - 2 * top, 1, 2 * top)


def outside(i, halo):
    if i == 0:
        return halo
    me = lax.axis_index("space")
    inside = jnp.logical_and(me > 0, me < lax.axis_size("space") - 1)
    return jnp.where(inside, halo, jnp.zeros_like(halo))


def edge_kernel(latent, near, far, sw, sb, tw, hidden, tw_v, sem):
    copy = pltpu.make_async_copy(tw, tw_v, sem)
    copy.start()
    for i, (halo, (r, beyond, _, order)) in enumerate(zip((near, far), sides(latent.shape[1]))):
        hidden[i] = activate([outside(i, halo[...]), latent[:, r], latent[:, beyond]], order, sw, sb[...])
    copy.wait()


def join_kernel(steps, latent, prev, corners, hidden, sw, sb, tw, tb, *rest):
    outs, mixed = rest[:-1], rest[-1]
    rows = latent.shape[1]
    me = lax.axis_index("space")
    before = [
        activate([outside(i, corners[i]), prev[:, r], prev[:, beyond]], order, sw, sb[...])
        for i, (r, beyond, _, order) in enumerate(sides(rows))
    ]
    for i, (r, _, place, _) in enumerate(sides(rows)):
        mixed[:, place] = mix(before[i], hidden[i], latent[:, r], tw, tb[...])
    for k, out in zip(steps, outs):
        out[...] = mixed[lax.bitwise_xor(me, k)]


def grow_kernel(plan, pieces, out, grown, sems):
    tile = out.shape[1] // lax.axis_size("space")
    cols = out.shape[2] // 2
    me = lax.axis_index("space")
    at = lax.broadcasted_iota(jnp.int32, (2 * cols, cols), 0)
    of = lax.broadcasted_iota(jnp.int32, (2 * cols, cols), 1)
    twice = jnp.where(at // 2 == of, 1.0, 0.0).astype(BF16)
    rows = [(piece, i) for piece in pieces for i in range(piece.shape[0])]
    copies, used = [], 0
    for src, k, runs in plan:
        src = lax.bitwise_xor(me, k) if src is None else src
        for first, count in runs:
            for i in range(count):
                piece, r = rows[used + i]
                wide = jnp.dot(twice, piece[r], preferred_element_type=jnp.float32).astype(BF16)
                grown[2 * (used + i)] = wide
                grown[2 * (used + i) + 1] = wide
            copy = pltpu.make_async_copy(
                grown.at[pl.ds(2 * used, 2 * count)],
                out.at[0, pl.ds(src * tile + 2 * first, 2 * count)],
                sems.at[len(copies)],
            )
            copy.start()
            copies.append(copy)
            used += count
    for copy in copies:
        copy.wait()


def grow(plan, pieces, out, height, name):
    cols, chans = pieces[0].shape[1:]
    count = sum(p.shape[0] for p in pieces)
    extra = [] if out is None else [out]
    m = len(pieces)
    return pl.pallas_call(
        lambda *refs: grow_kernel(plan, refs[:m], *refs[m + len(extra) :]),
        out_shape=bf16(1, 2 * height, 2 * cols, chans),
        in_specs=[VMEM] * m + [HBM] * len(extra),
        out_specs=HBM,
        input_output_aliases={m: 0} if extra else {},
        scratch_shapes=[
            pltpu.VMEM((2 * count, 2 * cols, chans), BF16),
            pltpu.SemaphoreType.DMA((sum(len(runs) for _, _, runs in plan),)),
        ],
        compiler_params=PARAMS,
        cost_estimate=pl.CostEstimate(flops=0, transcendentals=0, bytes_accessed=8 * count * cols * chans),
        name=name,
    )(*pieces, *extra)


def cost(rows, taps, chans):
    return pl.CostEstimate(flops=2 * taps * rows * chans * chans, transcendentals=rows * chans, bytes_accessed=2 * MIB)


def swap(block, k):
    return lax.ppermute(block, "space", [(i, i ^ k) for i in range(lax.axis_size("space"))])


def ahead(block):
    n = lax.axis_size("tm")
    return lax.ppermute(block, "tm", [(t, (t + 1) % n) for t in range(n)])


def beside(block):
    ts, n = lax.axis_size("tm"), lax.axis_size("space")
    route = []
    for t in range(ts):
        for s in range(n):
            to = (t ^ 1 if t ^ 1 < ts else t, s) if s in (0, n - 1) else (t, s + 1 if s % 2 else s - 1)
            route.append((t * n + s, to[0] * n + to[1]))
    return lax.ppermute(block, ("tm", "space"), route)


def body(latent, spatial_weight, spatial_bias, temporal_weight, temporal_bias):
    frames, rows, cols, chans = latent.shape
    n = lax.axis_size("space")
    if n & (n - 1) or frames != n:
        raise ValueError("shape")
    steps = exchanges(n)

    args = [latent, spatial_weight, spatial_bias.reshape(1, chans), temporal_weight, temporal_bias.reshape(1, chans)]
    args = [pltpu.with_memory_space_constraint(a, pltpu.HBM) for a in args]
    near, far, last = pl.pallas_call(
        border_kernel,
        out_shape=[bf16(frames, cols, chans), bf16(frames, cols, chans), bf16(2, rows, cols, chans)],
        in_specs=[HBM],
        out_specs=[VMEM] * 3,
        scratch_shapes=[pltpu.SemaphoreType.DMA((3,))],
        compiler_params=PARAMS,
        name="border",
    )(args[0])
    near = swap(near, 1)
    far = beside(far)
    prev = ahead(last)
    hidden, latent, *params = pl.pallas_call(
        inner_kernel,
        out_shape=[bf16(rows - 2, frames, cols, chans)] + [jax.ShapeDtypeStruct(a.shape, a.dtype) for a in args],
        in_specs=[HBM] * 5,
        out_specs=[VMEM] * 6,
        scratch_shapes=[pltpu.SemaphoreType.DMA((5,))],
        compiler_params=PARAMS,
        cost_estimate=cost(frames * (rows - 2) * cols, 9, chans),
        name="inner",
    )(*args)
    inner = pl.pallas_call(
        inner_mix_kernel,
        out_shape=bf16(frames, rows - 2, cols, chans),
        in_specs=[VMEM] * 7,
        out_specs=VMEM,
        compiler_params=PARAMS,
        cost_estimate=cost(frames * (rows - 2) * cols, 6, chans),
        name="inner_mix",
    )(latent, prev, hidden, *params)
    inner_own = inner
    inner = lax.all_to_all(inner, "space", split_axis=0, concat_axis=1, tiled=True)[0]

    near, far, token = lax.optimization_barrier((near, far, inner_own))
    corners = ahead(jnp.stack([near[frames - 2 :], far[frames - 2 :]]))
    hidden, tw = pl.pallas_call(
        edge_kernel,
        out_shape=[bf16(2, frames, cols, chans), bf16(*temporal_weight.shape)],
        in_specs=[VMEM] * 5 + [HBM],
        out_specs=[VMEM] * 2,
        scratch_shapes=[pltpu.SemaphoreType.DMA],
        compiler_params=PARAMS,
        cost_estimate=cost(frames * 2 * cols, 9, chans),
        name="edge",
    )(latent, near, far, *params[:2], args[3])
    edges = pl.pallas_call(
        lambda *refs: join_kernel([0] + steps, *refs),
        out_shape=[bf16(2, cols, chans)] * n,
        in_specs=[VMEM] * 8,
        out_specs=[VMEM] * n,
        scratch_shapes=[pltpu.VMEM((frames, 2, cols, chans), BF16)],
        compiler_params=PARAMS,
        cost_estimate=cost(frames * 2 * cols, 6, chans),
        name="join",
    )(latent, prev, corners, hidden, *params[:2], tw, params[3])
    edges = [edges[0]] + [swap(edge, k) for k, edge in zip(steps, edges[1:])]

    out = grow([(s, None, [(1, rows - 2)]) for s in range(n)], [pltpu.with_memory_space_constraint(inner, pltpu.HBM)], None, rows * n, "grow_inner")
    ends = [(0, 1), (rows - 1, 1)]
    cut = 2
    out = grow([(None, k, ends) for k in [0] + steps[:cut]], edges[: cut + 1], out, rows * n, "grow_first")
    return grow([(None, k, ends) for k in steps[cut:]], edges[cut + 1 :], out, rows * n, "grow_last")


def solution(mesh):
    in_specs = (P("tm", "space", None, None), P(), P(), P(), P())
    out_specs = P(("tm", "space"), None, None, None)
    return jax.shard_map(body, mesh=mesh, in_specs=in_specs, out_specs=out_specs, check_vma=False)
```
